1024 devices in a mesh: dp: 8 (over z_lo, core), hidden: 16 (over x, z_hi), mp: 8 (over y).
Axes of the slice: x: 8, y: 8, z: 8 (z_hi: 2, z_lo: 4; z = z_hi * 4 + z_lo), core: 2. Of those that a mesh axis runs over, the one named last changes fastest.
Arguments:
- activations: bfloat16 [4096, 26624], P('dp', 'hidden'), may hold values from -6 to 6
- weight: bfloat16 [26624, 8192], P('hidden', 'mp'), may hold values from -0.0390625 to 0.0390625
- out_grad: bfloat16 [4096, 8192], P(('dp', 'hidden'), 'mp'), may hold values from -0.25 to 0.25
- momentum: float32 [8, 3328, 8192], P('dp', 'hidden', 'mp'), may hold values from -6 to 6
Outputs:
- output: bfloat16 [4096, 8192], P(('dp', 'hidden'), 'mp')
- new_momentum: float32 [8, 3328, 8192], P('dp', 'hidden', 'mp')
- new_weight: bfloat16 [8, 3328, 8192], P('dp', 'hidden', 'mp')
The draws below stay inside these ranges and needn't reach their ends.
All inputs are finite; a program needn't handle non-finite values.
Results may differ from the reference program's by a relative error of at most 0.015.
Values may be sent and summed in bfloat16 or wider, within the bound.
No kernel may reach another device: no remote copies, remote signals or barrier semaphores. Data moves between devices by JAX's collectives and lax.ppermute only.
A program may use at most 32 MiB of HBM per device.

```python
import jax
import jax.numpy as jnp
from jax import lax

D = 8192
HID = 26624
TOK_DEV = 512
GROUPS = 8
HID_BLOCKS = 16
TOKENS = 4096
SLAB = 208
N_DP = 8


def levels(own_key, shape, pieces, low, top_value):
    def one(position, shards_of):
        steps = jax.random.uniform(jax.random.fold_in(jax.random.fold_in(own_key, 6), position), (shards_of,), jnp.float32, low / len(pieces), top_value / len(pieces))
        return jnp.repeat(jnp.exp(steps), shape[position] // shards_of).reshape((-1,) + (1,) * (len(shape) - position - 1))

    loudness = one(*pieces[0])
    for cut in pieces[1:]:
        loudness = loudness * one(*cut)
    return loudness


def scatter_about(key, shape, width, bound, pieces=(), held_as=jnp.bfloat16):
    factor_of = levels(key, shape, pieces, -0.22, 0.18) if pieces else 1.0
    drawn = jax.random.normal(key, shape, jnp.float32) * width * factor_of
    return jnp.minimum(jnp.maximum(drawn, -bound), bound).astype(held_as)


def setup_inputs(seed: int = 0) -> dict:
    keys = jax.random.split(jax.random.key(seed), 5)
    activations = scatter_about(keys[0], (TOKENS, HID), 1.0, 6.0, ((0, 8), (1, 16)))
    weight = scatter_about(keys[1], (HID, D), HID ** -0.5, 0.0390625, ((0, 16), (1, 8)))
    out_grad = scatter_about(keys[2], (TOKENS, D), ((TOK_DEV * N_DP) ** -0.5), 0.25, ((0, 128), (1, 8)))
    momentum = scatter_about(keys[3], (GROUPS, HID // GROUPS, D), 1.0, 6.0, ((0, 8), (1, 16), (2, 8)), jnp.float32)
    return {"activations": activations, "weight": weight, "out_grad": out_grad, "momentum": momentum}


momentum_decay = 0.9
step_size = 0.05


def stack_slabs(matrix):
    shaped = matrix.reshape(HID_BLOCKS, GROUPS, SLAB, D)
    return jnp.transpose(shaped, (1, 0, 2, 3)).reshape(GROUPS, HID // GROUPS, D)


def reference(activations, weight, out_grad, momentum):
    output = jnp.dot(activations, weight, preferred_element_type=jnp.float32).astype(jnp.bfloat16)

    def add_group(group, running):
        first_row = (group * TOK_DEV).astype(jnp.int32)
        act_rows = lax.dynamic_slice_in_dim(activations, first_row, TOK_DEV, 0)
        grad_rows = lax.dynamic_slice_in_dim(out_grad, first_row, TOK_DEV, 0)
        partial_value = lax.dot_general(act_rows, grad_rows, (((0,), (0,)), ((), ())), preferred_element_type=jnp.float32)
        return running + partial_value.astype(jnp.bfloat16).astype(jnp.float32)

    gradient = lax.fori_loop(0, GROUPS, add_group, jnp.zeros((HID, D), jnp.float32))
    new_momentum = momentum_decay * momentum + stack_slabs(gradient)
    new_weight = (stack_slabs(weight).astype(jnp.float32) - step_size * new_momentum).astype(jnp.bfloat16)
    return output, new_momentum, new_weight
```

```python
import jax
import jax.numpy as jnp
from jax import lax
from jax.sharding import PartitionSpec as P

momentum_decay = 0.9
step_size = 0.05


def on_device(activations, weight, out_grad, momentum):
    slab_rows = momentum.shape[1]
    tokens = activations.shape[0]
    own_tokens, cols = out_grad.shape
    blocks = tokens // own_tokens
    gathered = lax.all_to_all(
        jnp.broadcast_to(out_grad[None], (blocks, own_tokens, cols)),
        "hidden",
        split_axis=0,
        concat_axis=0,
        tiled=True,
    ).reshape(tokens, cols)
    local_grad = lax.dot_general(
        activations,
        gathered,
        (((0,), (0,)), ((), ())),
        preferred_element_type=jnp.float32,
    )
    grad_share = lax.psum_scatter(
        local_grad.astype(jnp.bfloat16), "dp", scatter_dimension=0, tiled=True
    ).astype(jnp.float32)
    partial_out = jnp.dot(activations, weight, preferred_element_type=jnp.float32)
    pieces = lax.all_to_all(
        partial_out.astype(jnp.bfloat16).reshape(blocks, own_tokens, cols),
        "hidden",
        split_axis=0,
        concat_axis=0,
        tiled=True,
    )
    summed = jnp.sum(pieces.astype(jnp.float32), axis=0).astype(jnp.bfloat16)
    new_momentum = momentum_decay * momentum + grad_share[None]
    own_rows = lax.dynamic_slice_in_dim(weight, lax.axis_index("dp") * slab_rows, slab_rows, 0)
    new_weight = (own_rows.astype(jnp.float32)[None] - step_size * new_momentum).astype(
        jnp.bfloat16
    )
    return (summed, new_momentum, new_weight)


def solution(mesh):
    placed = (
        P("dp", "hidden"),
        P("hidden", "mp"),
        P(("dp", "hidden"), "mp"),
        P("dp", "hidden", "mp"),
    )
    return jax.shard_map(
        on_device,
        mesh=mesh,
        in_specs=placed,
        out_specs=(P(("dp", "hidden"), "mp"), P("dp", "hidden", "mp"), P("dp", "hidden", "mp")),
        check_vma=False,
    )
```

```python
import jax
import jax.numpy as jnp
import numpy as np
from jax import lax
from jax.sharding import Mesh, PartitionSpec as P

momentum_decay = 0.9
step_size = 0.05

PARTS = 2
SWAP = [(0, 1), (1, 0)]


def after(value, *others):
    return lax.optimization_barrier((value, *others))[0]


def on_device(activations, weight, out_grad, momentum):
    slab_rows = momentum.shape[1]
    tokens, hid = activations.shape
    own_tokens, cols = out_grad.shape
    blocks = tokens // own_tokens
    half = cols // 2
    part = half // PARTS
    core, z_hi, z_lo = (lax.axis_index(a) for a in ("core", "z_hi", "z_lo"))
    n_z = hid // slab_rows // 2

    mine = lax.dynamic_slice_in_dim(out_grad, core * half, half, 1)
    other = lax.dynamic_slice_in_dim(out_grad, (1 - core) * half, half, 1)
    pair = jnp.stack([mine, lax.ppermute(other, "core", SWAP)])
    sends = [
        jnp.broadcast_to(pair[None, :, :, p * part : (p + 1) * part], (blocks, 2, own_tokens, part))
        for p in range(PARTS)
    ]
    gathered = []
    for sent in sends:
        if gathered:
            sent = after(sent, gathered[-1])
        gathered.append(
            lax.all_to_all(sent, ("x", "z_hi"), split_axis=0, concat_axis=0, tiled=True)
        )

    partner_act = lax.ppermute(after(activations, sends[0]), "core", SWAP)
    both_act = jnp.stack(
        [activations.reshape(blocks, own_tokens, hid), partner_act.reshape(blocks, own_tokens, hid)],
        axis=1,
    ).reshape(2 * tokens, hid)

    partial_out = jnp.dot(activations, weight, preferred_element_type=jnp.float32)
    partial_out = partial_out.astype(jnp.bfloat16).reshape(blocks // 2, 2, own_tokens, cols)
    keep = lax.dynamic_index_in_dim(partial_out, z_hi, 1, keepdims=False)
    give = lax.dynamic_index_in_dim(partial_out, 1 - z_hi, 1, keepdims=False)
    got = lax.ppermute(give, "z_hi", SWAP)
    paired = (keep.astype(jnp.float32) + got.astype(jnp.float32)).astype(jnp.bfloat16)
    pieces = lax.all_to_all(
        after(paired, gathered[-1]), "x", split_axis=0, concat_axis=0, tiled=True
    )
    summed = jnp.sum(pieces.astype(jnp.float32), axis=0).astype(jnp.bfloat16)

    own_piece, arrived = [], []
    for p in range(PARTS):
        local_grad = lax.dot_general(
            both_act,
            gathered[p].reshape(2 * tokens, part),
            (((0,), (0,)), ((), ())),
            preferred_element_type=jnp.float32,
        )
        slabs = local_grad.astype(jnp.bfloat16).reshape(n_z, 2, slab_rows, part)
        own_piece.append(lax.dynamic_index_in_dim(slabs, z_lo, 0, keepdims=False))
        sent = [
            lax.dynamic_index_in_dim(slabs, (z_lo + d) % n_z, 0, keepdims=False)
            for d in range(1, n_z)
        ]
        if p > 0:
            arrived[-1] = list(lax.optimization_barrier((*arrived[-1], sent[0]))[:-1])
        arrived.append(
            [
                lax.ppermute(s, "z_lo", [(i, (i + d) % n_z) for i in range(n_z)])
                for d, s in enumerate(sent, 1)
            ]
        )
    own_part, got_part = [], []
    for own, others in zip(own_piece, arrived):
        total = own.astype(jnp.float32)
        for a in others:
            total = total + a.astype(jnp.float32)
        own_part.append(lax.dynamic_index_in_dim(total, core, 0, keepdims=False))
        give = lax.dynamic_index_in_dim(total, 1 - core, 0, keepdims=False).astype(jnp.bfloat16)
        got_part.append(lax.ppermute(give, "core", SWAP).astype(jnp.float32))
    own_half = jnp.concatenate(own_part, axis=1)
    got_half = jnp.concatenate(got_part, axis=1)
    grad_share = jnp.concatenate(
        [jnp.where(core == 0, own_half, got_half), jnp.where(core == 0, got_half, own_half)], axis=1
    )
    new_momentum = momentum_decay * momentum + grad_share[None]
    own_rows = lax.dynamic_slice_in_dim(weight, (z_lo * 2 + core) * slab_rows, slab_rows, 0)
    new_weight = (own_rows.astype(jnp.float32)[None] - step_size * new_momentum).astype(
        jnp.bfloat16
    )
    return (summed, new_momentum, new_weight)


def solution(mesh):
    n_dp, n_hidden, n_mp = (mesh.shape[a] for a in ("dp", "hidden", "mp"))
    grid = np.asarray(mesh.devices).reshape(n_dp // 2, 2, n_hidden // 2, 2, n_mp)
    finer = Mesh(grid, ("z_lo", "core", "x", "z_hi", "mp"))
    dp, hidden = ("z_lo", "core"), ("x", "z_hi")
    return jax.shard_map(
        on_device,
        mesh=finer,
        in_specs=(P(dp, hidden), P(hidden, "mp"), P(dp + hidden, "mp"), P(dp, hidden, "mp")),
        out_specs=(P(dp + hidden, "mp"), P(dp, hidden, "mp"), P(dp, hidden, "mp")),
        check_vma=False,
    )
```

```python
import jax
import jax.numpy as jnp
import numpy as np
from jax import lax
from jax.sharding import Mesh, PartitionSpec as P


momentum_decay = 0.9
step_size = 0.05

SWAP = [(0, 1), (1, 0)]


def after(value, *others):
    return lax.optimization_barrier((value, *others))[0]


def in_order(index, mine, other, axis):
    first, second = jnp.where(index == 0, mine, other), jnp.where(index == 0, other, mine)
    return jnp.stack([first, second], axis=axis)


def step(activations, weight, out_grad, momentum):
    slab_rows = momentum.shape[1]
    tokens, hid = activations.shape
    own_tokens, cols = out_grad.shape
    n_x = tokens // own_tokens // 2
    half = cols // 2
    part = half // 2
    core, z_hi, z_lo = (lax.axis_index(a) for a in ("core", "z_hi", "z_lo"))
    n_z = hid // slab_rows // 2

    sent = out_grad.reshape(own_tokens, 2, 2, part)[:, :, 0].transpose(1, 0, 2)
    sent = jnp.broadcast_to(sent[None, :, None], (n_x, 2, 2, own_tokens, part))
    gathered0 = lax.all_to_all(
        sent.reshape(4 * n_x, own_tokens, part),
        ("x", "core", "z_hi"),
        split_axis=0,
        concat_axis=0,
        tiled=True,
    )

    def second_part(of_core):
        return lax.dynamic_slice_in_dim(out_grad, of_core * half + part, part, 1)

    partner = lax.ppermute(second_part(1 - core), "core", SWAP)
    pair = in_order(core, second_part(core), partner, 0)
    far_pair = lax.ppermute(pair, "z_hi", SWAP)
    quad = in_order(z_hi, pair, far_pair, 1)
    sent = jnp.broadcast_to(quad[None], (n_x, 2, 2, own_tokens, part))
    gathered1 = lax.all_to_all(after(sent, gathered0), "x", split_axis=0, concat_axis=0, tiled=True)

    partner_act = lax.ppermute(after(activations, partner), "core", SWAP)
    both_act = in_order(
        core,
        activations.reshape(n_x, 2 * own_tokens, hid),
        partner_act.reshape(n_x, 2 * own_tokens, hid),
        1,
    ).reshape(2 * tokens, hid)
    both_act = lax.optimization_barrier(both_act)

    partial_out = jnp.dot(activations, weight, preferred_element_type=jnp.float32)
    partial_out = partial_out.astype(jnp.bfloat16).reshape(n_x, 2, own_tokens, cols)
    keep = lax.dynamic_index_in_dim(partial_out, z_hi, 1, keepdims=False)
    give = lax.dynamic_index_in_dim(partial_out, 1 - z_hi, 1, keepdims=False)
    got = lax.ppermute(after(give, far_pair), "z_hi", SWAP)

    own_piece, arrived = [], []
    for p, gathered in enumerate((gathered0, gathered1)):
        local_grad = lax.dot_general(
            both_act,
            gathered.reshape(2 * tokens, part),
            (((0,), (0,)), ((), ())),
            preferred_element_type=jnp.float32,
        )
        slabs = local_grad.astype(jnp.bfloat16).reshape(n_z, 2, slab_rows, part)
        own_piece.append(lax.dynamic_index_in_dim(slabs, z_lo, 0, keepdims=False))
        sent = [
            lax.dynamic_index_in_dim(slabs, (z_lo + d) % n_z, 0, keepdims=False)
            for d in range(1, n_z)
        ]
        if p > 0:
            arrived[-1] = list(lax.optimization_barrier((*arrived[-1], sent[0]))[:-1])
        arrived.append(
            [
                lax.ppermute(s, "z_lo", [(i, (i + d) % n_z) for i in range(n_z)])
                for d, s in enumerate(sent, 1)
            ]
        )
    got = after(got, sent[0])
    paired = (keep.astype(jnp.float32) + got.astype(jnp.float32)).astype(jnp.bfloat16)
    pieces = lax.all_to_all(paired, "x", split_axis=0, concat_axis=0, tiled=True)
    summed = jnp.sum(pieces.astype(jnp.float32), axis=0).astype(jnp.bfloat16)

    own_part, got_part = [], []
    for own, others in zip(own_piece, arrived):
        total = own.astype(jnp.float32)
        for a in others:
            total = total + a.astype(jnp.float32)
        own_part.append(lax.dynamic_index_in_dim(total, core, 0, keepdims=False))
        give = lax.dynamic_index_in_dim(total, 1 - core, 0, keepdims=False).astype(jnp.bfloat16)
        got_part.append(lax.ppermute(give, "core", SWAP).astype(jnp.float32))
    own_half = jnp.concatenate(own_part, axis=1)
    got_half = jnp.concatenate(got_part, axis=1)
    grad_share = jnp.concatenate(
        [jnp.where(core == 0, own_half, got_half), jnp.where(core == 0, got_half, own_half)], axis=1
    )
    new_momentum = momentum_decay * momentum + grad_share[None]
    own_rows = lax.dynamic_slice_in_dim(weight, (z_lo * 2 + core) * slab_rows, slab_rows, 0)
    new_weight = (own_rows.astype(jnp.float32)[None] - step_size * new_momentum).astype(
        jnp.bfloat16
    )
    return (summed, new_momentum, new_weight)


def solution(mesh):
    n_dp, n_hidden, n_mp = (mesh.shape[a] for a in ("dp", "hidden", "mp"))
    grid = np.asarray(mesh.devices).reshape(n_dp // 2, 2, n_hidden // 2, 2, n_mp)
    finer = Mesh(grid, ("z_lo", "core", "x", "z_hi", "mp"))
    dp, hidden = ("z_lo", "core"), ("x", "z_hi")
    return jax.shard_map(
        step,
        mesh=finer,
        in_specs=(P(dp, hidden), P(hidden, "mp"), P(dp + hidden, "mp"), P(dp, hidden, "mp")),
        out_specs=(P(dp + hidden, "mp"), P(dp, hidden, "mp"), P(dp, hidden, "mp")),
        check_vma=False,
    )
```

```python
import jax
import jax.numpy as jnp
import numpy as np
from jax import lax
from jax.sharding import Mesh, PartitionSpec as P


momentum_decay = 0.9
step_size = 0.05

SWAP = [(0, 1), (1, 0)]


def after(value, *others):
    return lax.optimization_barrier((value, *others))[0]


def placed(index, mine, other, axis, shape):
    return jnp.where(lax.broadcasted_iota(jnp.int32, shape, axis) == index, mine, other)


def halves(arrays, index):
    def entry(i):
        at = (lax.dynamic_index_in_dim(a, i, 0, keepdims=False) for a in arrays)
        return sum(a.astype(jnp.float32) for a in at)

    return lax.optimization_barrier((entry(index), entry(1 - index).astype(jnp.bfloat16)))


def step(activations, weight, out_grad, momentum):
    slab_rows = momentum.shape[1]
    tokens, hid = activations.shape
    own_tokens, cols = out_grad.shape
    n_x = tokens // own_tokens // 2
    half = cols // 2
    part = half // 2
    core, z_hi, z_lo = (lax.axis_index(a) for a in ("core", "z_hi", "z_lo"))

    mine = lax.dynamic_slice_in_dim(out_grad, core * half, half, 1)
    other = lax.dynamic_slice_in_dim(out_grad, (1 - core) * half, half, 1)
    partner = lax.ppermute(other, "core", SWAP)
    pair = placed(core, mine, partner, 0, (2, own_tokens, half))
    far = lax.ppermute(pair, "z_hi", SWAP)
    shape = (n_x, 2, 2, own_tokens, part)
    gathered = []
    for p in range(2):
        near_p, far_p = (a[None, :, None, :, p * part : (p + 1) * part] for a in (pair, far))
        sent = placed(z_hi, near_p, far_p, 2, shape)
        if p == 0:
            pair, far = lax.optimization_barrier((pair, far, sent))[:2]
        else:
            sent = after(sent, gathered[0])
        gathered.append(lax.all_to_all(sent, "x", split_axis=0, concat_axis=0, tiled=True))

    partner_act = lax.ppermute(activations, "core", SWAP)
    both_act = placed(
        core,
        activations.reshape(n_x, 1, 2 * own_tokens, hid),
        partner_act.reshape(n_x, 1, 2 * own_tokens, hid),
        1,
        (n_x, 2, 2 * own_tokens, hid),
    ).reshape(2 * tokens, hid)
    both_act = lax.optimization_barrier(both_act)

    partial_out = jnp.dot(activations, weight, preferred_element_type=jnp.float32)
    partial_out = partial_out.astype(jnp.bfloat16).reshape(n_x, 2, own_tokens, cols)
    keep_out = lax.dynamic_index_in_dim(partial_out, z_hi, 1, keepdims=False)
    give_out = lax.dynamic_index_in_dim(partial_out, 1 - z_hi, 1, keepdims=False)
    got_out = lax.ppermute(after(give_out, far), "z_hi", SWAP)

    def product(rows):
        local_grad = lax.dot_general(
            both_act,
            rows.reshape(2 * tokens, part),
            (((0,), (0,)), ((), ())),
            preferred_element_type=jnp.float32,
        )
        return local_grad.astype(jnp.bfloat16)

    bits = (z_lo // 2, z_lo % 2)
    slabs = product(gathered[0]).reshape(2, 2, 2, slab_rows, part)
    keep = lax.dynamic_index_in_dim(slabs, bits[1], 1, keepdims=False)
    give = lax.dynamic_index_in_dim(slabs, 1 - bits[1], 1, keepdims=False)
    keep, give = lax.optimization_barrier((keep, give))
    got = lax.ppermute(give, "z_lo", [(i, i ^ 1) for i in range(4)])
    slabs = product(after(gathered[1], give)).reshape(4, 2, slab_rows, part)
    keep, give = halves((keep, got), bits[0])
    got = lax.ppermute(give, "z_lo", [(i, i ^ 2) for i in range(4)])
    pieces = lax.optimization_barrier(
        tuple(lax.dynamic_index_in_dim(slabs, (z_lo + d) % 4, 0, keepdims=False) for d in range(4))
    )
    arrived = [
        lax.ppermute(pieces[d], "z_lo", [(i, (i + d) % 4) for i in range(4)]) for d in (1, 2, 3)
    ]
    own_part, got_part = [], []
    keep, give = halves((keep, got), core)
    own_part.append(keep)
    got_part.append(give)
    keep, give = halves((after(pieces[0], give), *arrived), core)
    own_part.append(keep)
    got_part.append(give)
    got = lax.ppermute(jnp.concatenate(got_part, axis=1), "core", SWAP).astype(jnp.float32)
    own = jnp.concatenate(own_part, axis=1)

    paired = (keep_out.astype(jnp.float32) + got_out.astype(jnp.float32)).astype(jnp.bfloat16)
    pieces = lax.all_to_all(
        after(paired, gathered[1]), "x", split_axis=0, concat_axis=0, tiled=True
    )
    summed = jnp.sum(pieces.astype(jnp.float32), axis=0).astype(jnp.bfloat16)

    grad_share = jnp.concatenate(
        [jnp.where(core == 0, own, got), jnp.where(core == 0, got, own)], axis=1
    )
    new_momentum = momentum_decay * momentum + grad_share[None]
    own_rows = lax.dynamic_slice_in_dim(weight, (z_lo * 2 + core) * slab_rows, slab_rows, 0)
    new_weight = (own_rows.astype(jnp.float32)[None] - step_size * new_momentum).astype(
        jnp.bfloat16
    )
    return (summed, new_momentum, new_weight)


def solution(mesh):
    n_dp, n_hidden, n_mp = (mesh.shape[a] for a in ("dp", "hidden", "mp"))
    grid = np.asarray(mesh.devices).reshape(n_dp // 2, 2, n_hidden // 2, 2, n_mp)
    finer = Mesh(grid, ("z_lo", "core", "x", "z_hi", "mp"))
    dp, hidden = ("z_lo", "core"), ("x", "z_hi")
    return jax.shard_map(
        step,
        mesh=finer,
        in_specs=(P(dp, hidden), P(hidden, "mp"), P(dp + hidden, "mp"), P(dp, hidden, "mp")),
        out_specs=(P(dp + hidden, "mp"), P(dp, hidden, "mp"), P(dp, hidden, "mp")),
        check_vma=False,
    )
```

```python
import jax
import jax.numpy as jnp
import numpy as np
from jax import lax
from jax.sharding import Mesh, PartitionSpec as P


momentum_decay = 0.9
step_size = 0.05

SWAP = [(0, 1), (1, 0)]


def after(value, *others):
    return lax.optimization_barrier((value, *others))[0]


def placed(index, mine, other, axis, shape):
    return jnp.where(lax.broadcasted_iota(jnp.int32, shape, axis) == index, mine, other)


def halves(mine, other, index):
    def entry(i):
        at = (lax.dynamic_index_in_dim(a, i, 0, keepdims=False) for a in (mine, other))
        return sum(a.astype(jnp.float32) for a in at)

    return lax.optimization_barrier((entry(index), entry(1 - index).astype(jnp.bfloat16)))


def step(activations, weight, out_grad, momentum):
    slab_rows = momentum.shape[1]
    tokens, hid = activations.shape
    own_tokens, cols = out_grad.shape
    n_x = tokens // own_tokens // 2
    half = cols // 2
    part = half // 2
    core, z_hi, z_lo = (lax.axis_index(a) for a in ("core", "z_hi", "z_lo"))

    shape = (n_x, 2, 2, own_tokens, part)
    sent = placed(0, out_grad[:, :part], out_grad[:, part : 2 * part], 1, shape)
    gathered0 = lax.all_to_all(
        sent.reshape(4 * n_x, own_tokens, part),
        ("x", "core", "z_hi"),
        split_axis=0,
        concat_axis=0,
        tiled=True,
    )

    far = lax.ppermute(out_grad[:, 2 * part :], "z_hi", SWAP)
    by_core = [
        placed(z_hi, out_grad[:, 2 * part :][:, c], far[:, c], 2, shape)
        for c in (slice(0, part), slice(part, 2 * part))
    ]
    sent = placed(0, *by_core, 1, shape)
    gathered1 = lax.all_to_all(
        after(sent, gathered0).reshape(2 * n_x, 2, own_tokens, part),
        ("x", "core"),
        split_axis=0,
        concat_axis=0,
        tiled=True,
    )

    partner_act = lax.ppermute(activations, "core", SWAP)
    both_act = placed(
        core,
        activations.reshape(n_x, 1, 2 * own_tokens, hid),
        partner_act.reshape(n_x, 1, 2 * own_tokens, hid),
        1,
        (n_x, 2, 2 * own_tokens, hid),
    ).reshape(2 * tokens, hid)
    both_act = lax.optimization_barrier(both_act)

    partial_out = jnp.dot(activations, weight, preferred_element_type=jnp.float32)
    partial_out = partial_out.astype(jnp.bfloat16).reshape(n_x, 2, own_tokens, cols)
    keep_out = lax.dynamic_index_in_dim(partial_out, z_hi, 1, keepdims=False)
    give = lax.dynamic_index_in_dim(partial_out, 1 - z_hi, 1, keepdims=False)
    got_out = lax.ppermute(after(give, far), "z_hi", SWAP)

    bits = (z_lo // 2, z_lo % 2)
    own_part, got_part = [], []
    for p, gathered in enumerate((gathered0, gathered1)):
        if p > 0:
            gathered = after(gathered, cut)
        local_grad = lax.dot_general(
            both_act,
            gathered.reshape(2 * tokens, part),
            (((0,), (0,)), ((), ())),
            preferred_element_type=jnp.float32,
        )
        slabs = local_grad.astype(jnp.bfloat16).reshape(2, 2, 2, slab_rows, part)
        keep = lax.dynamic_index_in_dim(slabs, bits[1], 1, keepdims=False)
        give = lax.dynamic_index_in_dim(slabs, 1 - bits[1], 1, keepdims=False)
        keep, give = lax.optimization_barrier((keep, give))
        cut = give
        got = lax.ppermute(give, "z_lo", [(i, i ^ 1) for i in range(4)])
        if p > 0:
            keep = after(keep, mid)
        keep, give = halves(keep, got, bits[0])
        mid = give
        got = lax.ppermute(give, "z_lo", [(i, i ^ 2) for i in range(4)])
        if p > 0:
            keep = after(keep, end)
        keep, give = halves(keep, got, core)
        end = give
        own_part.append(keep)
        got_part.append(lax.ppermute(give, "core", SWAP).astype(jnp.float32))

    paired = (keep_out.astype(jnp.float32) + got_out.astype(jnp.float32)).astype(jnp.bfloat16)
    pieces = lax.all_to_all(after(paired, gathered1), "x", split_axis=0, concat_axis=0, tiled=True)
    summed = jnp.sum(pieces.astype(jnp.float32), axis=0).astype(jnp.bfloat16)

    grad_share = jnp.concatenate(
        [
            piece
            for own, got in zip(own_part, got_part)
            for piece in (jnp.where(core == 0, own, got), jnp.where(core == 0, got, own))
        ],
        axis=1,
    )
    new_momentum = momentum_decay * momentum + grad_share[None]
    own_rows = lax.dynamic_slice_in_dim(weight, (z_lo * 2 + core) * slab_rows, slab_rows, 0)
    new_weight = (own_rows.astype(jnp.float32)[None] - step_size * new_momentum).astype(
        jnp.bfloat16
    )
    return (summed, new_momentum, new_weight)


def solution(mesh):
    n_dp, n_hidden, n_mp = (mesh.shape[a] for a in ("dp", "hidden", "mp"))
    grid = np.asarray(mesh.devices).reshape(n_dp // 2, 2, n_hidden // 2, 2, n_mp)
    finer = Mesh(grid, ("z_lo", "core", "x", "z_hi", "mp"))
    dp, hidden = ("z_lo", "core"), ("x", "z_hi")
    return jax.shard_map(
        step,
        mesh=finer,
        in_specs=(P(dp, hidden), P(hidden, "mp"), P(dp + hidden, "mp"), P(dp, hidden, "mp")),
        out_specs=(P(dp + hidden, "mp"), P(dp, hidden, "mp"), P(dp, hidden, "mp")),
        check_vma=False,
    )
```
